512 devices in a mesh: sub: 512 (over y, z, x, core).
Axes of the slice: x: 4, y: 4, z: 16, core: 2. Of those that a mesh axis runs over, the one named last changes fastest.
Arguments:
- right_side: bfloat16 [512, 1024, 128], P('sub'), may hold values from -6 to 6
- schur: bfloat16 [512, 1024, 1024], P('sub'), may hold values from -1 to 2
- neumann: bfloat16 [512, 1024, 1024], P('sub'), may hold values from -1 to 1
- weights: float32 [512, 1024], P('sub'), may hold values from 0.25 to 1
- neighbours: int32 [512, 4], P('sub'), may hold values from -1 to 511, as said below
- counts: int32 [512], P('sub'), may hold values from 512 to 1024, as said below
- shared_rows: int32 [512, 4, 128], P('sub'), may hold values from 0 to 1023, as said below
Outputs:
- solution: float32 [512, 1024, 128], P('sub')
The draws below stay inside these ranges and needn't reach their ends.
Inputs may be any that keep to these rules, and one draw needn't show every extreme that they name: `neighbours`: slot 0 holds s + 1, slot 1 s - 1, slot 2 s + 16, slot 3 s - 16 where that link exists, else -1; links are symmetric: s names t in a slot exactly when t names s in the opposite slot. Subdomains 512 - 2 and 511 are always linked. `counts`: every subdomain has at least 512 nodes in use; some subdomain uses all 1024. `shared_rows`: every entry of subdomain s is below counts[s]; entries of one list may repeat.
All inputs are finite; a program needn't handle non-finite values.
Results may differ from the reference program's by a relative error of at most 0.0075.
Values may be sent and summed in bfloat16 or wider, within the bound.
A program may use at most 64 MiB of HBM per device.

```python
import math
import jax
import jax.numpy as jnp
from jax import lax

NI = 1024
LEADS = 128
SHARE = 128
ITERS = 4
SUBS = 512


def common_counts(key):
    base = jax.random.randint(jax.random.fold_in(key, 11), (SUBS,), NI // 2, NI + 1)
    top = jax.random.randint(jax.random.fold_in(key, 12), (), 0, SUBS)
    base = base.at[top].set(NI)
    base = base.at[(top + 1) % SUBS].set(NI // 2)
    return (base.astype(jnp.int32), top)


def draw_counts(key, part):
    used, top = common_counts(key)
    return used


def draw_shared_rows(key, part):
    used, top = common_counts(key)
    raw = jax.random.randint(jax.random.fold_in(key, 13), (SUBS, 4, SHARE), 0, 1048576)
    rows = (raw % used[:, None, None]).astype(jnp.int32)
    rows = rows.at[top, 0, 0].set(NI - 1)
    rows = rows.at[top, 0, 1].set(0)
    return rows.astype(jnp.int32)


def draw_neighbours(key, part):
    index = jnp.arange(SUBS)
    near = (jax.random.randint(jax.random.fold_in(key, 21), (SUBS,), 0, 4) < 3) & (index + 1 < SUBS)
    near = near | (index == SUBS - 2)
    far = (jax.random.randint(jax.random.fold_in(key, 22), (SUBS,), 0, 4) < 3) & (index + 16 < SUBS)
    slot_up = jnp.where(near, index + 1, -1)
    slot_down = jnp.where(jnp.roll(near, 1) & (index >= 1), index - 1, -1)
    slot_far_up = jnp.where(far, index + 16, -1)
    slot_far_down = jnp.where(jnp.roll(far, 16) & (index >= 16), index - 16, -1)
    return jnp.stack([slot_up, slot_down, slot_far_up, slot_far_down], 1).astype(jnp.int32)


def dominant(key, spread, low, high):
    shape = (SUBS, NI, NI)
    off = jax.random.normal(jax.random.fold_in(key, 1), shape, jnp.float32) * (spread / math.sqrt(NI))
    diag = jax.random.uniform(jax.random.fold_in(key, 2), (SUBS, NI, 1), jnp.float32, low, high)
    eye = (jnp.arange(NI)[:, None] == jnp.arange(NI)[None, :]).astype(jnp.float32)
    return (off * (1.0 - eye) + eye * diag).astype(jnp.bfloat16)


def draw_schur(key, part):
    return dominant(jax.random.fold_in(key, 31), 0.25, 1.0, 2.0)


def draw_neumann(key, part):
    return dominant(jax.random.fold_in(key, 32), 0.15, 0.5, 1.0)


def block_levels(stream_key, shape, pieces, smallest, high):
    loudness = 1.0
    for position, blocks in pieces:
        draws = jax.random.uniform(jax.random.fold_in(jax.random.fold_in(stream_key, 6), position), (blocks,), jnp.float32, smallest / len(pieces), high / len(pieces))
        loudness = loudness * jnp.repeat(jnp.exp(draws), shape[position] // blocks).reshape((-1,) + (1,) * (len(shape) - 1 - position))
    return loudness


def centred(own_key, dims, scale, most, shards=(), kind=jnp.bfloat16):
    loudness = block_levels(own_key, dims, shards, -0.22, 0.18) if shards else 1.0
    result = jax.random.normal(own_key, dims, jnp.float32) * scale * loudness
    return jnp.minimum(jnp.maximum(result, -most), most).astype(kind)


def setup_inputs(seed: int = 0) -> dict:
    key_of = jax.random.split(jax.random.key(seed), 8)
    right_side = centred(key_of[0], (SUBS, NI, LEADS), 1.0, 6.0, ((0, 512),))
    schur = draw_schur(jax.random.fold_in(key_of[7], 71), 0)
    neumann = draw_neumann(jax.random.fold_in(key_of[7], 71), 0)
    weights = jnp.clip(jnp.exp(math.log(1.0) - 1.3862944 * jax.random.uniform(key_of[3], (SUBS, NI), jnp.float32) ** block_levels(key_of[3], (SUBS, NI), ((0, 512),), -0.2, 0.2)), 0.25, 1.0)
    neighbours = draw_neighbours(jax.random.fold_in(key_of[7], 71), 0)
    counts = draw_counts(jax.random.fold_in(key_of[7], 71), 0)
    shared_rows = draw_shared_rows(jax.random.fold_in(key_of[7], 71), 0)
    return dict(right_side=right_side, schur=schur, neumann=neumann, weights=weights, neighbours=neighbours, counts=counts, shared_rows=shared_rows)


link_offsets = (1, -1, 16, -16)
opposite_slot = (1, 0, 3, 2)
damping_factor = 0.7


def shift_rows(packed, offset):
    total_subs = packed.shape[0]
    padding = jnp.zeros((abs(offset),) + packed.shape[1:], packed.dtype)
    if offset > 0:
        return jnp.concatenate([packed[offset:], padding], 0)
    return jnp.concatenate([padding, packed[:total_subs + offset]], 0)


def assemble(own, sent, shared_rows, live):
    total = own
    sub_index = jnp.arange(own.shape[0])[:, None]
    for slot in range(4):
        packed = sent[sub_index, shared_rows[:, opposite_slot[slot]]]
        received = shift_rows(packed, link_offsets[slot]).astype(jnp.float32)
        received = received * live[:, slot][:, None, None]
        total = total.at[sub_index, shared_rows[:, slot]].add(received)
    return total


def reference(right_side, schur, neumann, weights, neighbours, counts, shared_rows):
    width = schur.shape[1]
    mask = (jnp.arange(width)[None, :] < counts[:, None]).astype(jnp.float32)[:, :, None]
    live = (neighbours >= 0).astype(jnp.float32)
    weight = weights[:, :, None]
    rhs = right_side.astype(jnp.float32)
    solution = jnp.zeros(right_side.shape, jnp.float32)
    for step in range(ITERS):
        current = solution.astype(jnp.bfloat16)
        product = lax.map(lambda pair: jnp.dot(pair[0].T, pair[1], preferred_element_type=jnp.float32), (schur, current))
        local = mask * (rhs - product)
        residual = assemble(local, local.astype(jnp.bfloat16), shared_rows, live)
        scaled = (weight * residual).astype(jnp.bfloat16)
        correction = lax.map(lambda pair: jnp.dot(pair[0], pair[1], preferred_element_type=jnp.float32), (neumann, scaled))
        weighted = mask * weight * correction
        update = assemble(weighted, weighted.astype(jnp.bfloat16), shared_rows, live)
        solution = solution + damping_factor * update
    return solution
```

```python
import functools

import jax
import jax.numpy as jnp
from jax import lax
from jax.experimental import pallas as pl
from jax.experimental.pallas import tpu as pltpu
from jax.sharding import PartitionSpec as P

ITERS = 4
OFFSETS = (1, -1, 16, -16)
OPPOSITE = (1, 0, 3, 2)
SEND_ORDER = (2, 3, 0, 1)
DAMPING = 0.7
F32, BF16 = jnp.float32, jnp.bfloat16


def mm(a, b):
    return jnp.dot(a, b, preferred_element_type=F32)


def mm_t(a, b):
    return lax.dot_general(a, b, (((1,), (1,)), ((), ())), preferred_element_type=F32)


def kernel(
    n, rhs_hbm, s_hbm, n_hbm, w_ref, nb_ref, cnt_ref, rows_ref, out_ref,
    rhs, s_mat, n_mat, st, et, el, gs, gse, gn, gne, wm, w_e, p0, t, x, u, wlb,
    send, recv, load_sem, send_sem, recv_sem,
):
    width, leads = rhs.shape
    share = rows_ref.shape[2]
    links = 4 * share
    me = lax.axis_index("sub")
    partner = [lax.rem(me + (o + n), n) for o in OFFSETS]

    loads = [
        pltpu.make_async_copy(rhs_hbm.at[0], rhs, load_sem.at[0]),
        pltpu.make_async_copy(n_hbm.at[0], n_mat, load_sem.at[1]),
        pltpu.make_async_copy(s_hbm.at[0], s_mat, load_sem.at[2]),
    ]
    for copy in loads:
        copy.start()

    barrier = pltpu.get_barrier_semaphore()
    for to in partner:
        pl.semaphore_signal(barrier, inc=1, device_id=(to,), device_id_type=pl.DeviceIdType.MESH)

    def copy_of(e, slot):
        there = OPPOSITE[slot]
        return pltpu.make_async_remote_copy(
            src_ref=send.at[e, pl.ds(slot * share, share)],
            dst_ref=recv.at[e, pl.ds(there * share, share)],
            send_sem=send_sem.at[e, slot],
            recv_sem=recv_sem.at[e, there],
            device_id=(partner[slot],),
            device_id_type=pl.DeviceIdType.MESH,
        )

    def part(slot):
        return slice(slot * share, (slot + 1) * share)

    row_of = lax.broadcasted_iota(jnp.int32, (width, share), 0)
    lane_of = lax.broadcasted_iota(jnp.int32, (share, width), 1)
    for slot in range(4):
        rows = rows_ref[0, slot : slot + 1, :]
        column = jnp.transpose(jnp.broadcast_to(rows, (share, share)))[:, :1]
        hit = lane_of == column
        et[part(slot), :] = hit.astype(F32).astype(BF16)
        live = (nb_ref[0, slot] >= 0).astype(F32)
        el[:, part(slot)] = (jnp.where(row_of == rows, 1.0, 0.0) * live).astype(BF16)
        mine = jnp.sum(jnp.where(hit, w_ref[0:1, :], 0.0), axis=1, keepdims=True)
        w_e[part(slot), :] = jnp.broadcast_to(mine, (share, leads))

    loads[0].wait()
    first = mm(et[...], rhs[...])
    p0[...] = first
    send[0] = first.astype(BF16)
    pl.semaphore_wait(barrier, 4)
    for slot in SEND_ORDER:
        copy_of(0, slot).start()

    count = cnt_ref[0]
    for block in range(width // 128):
        at = slice(block * 128, (block + 1) * 128)
        w_col = jnp.transpose(jnp.broadcast_to(w_ref[0:1, at], (128, 128)))
        used = lax.broadcasted_iota(jnp.int32, (128, 128), 0) + block * 128 < count
        wm[at, :] = jnp.where(used, w_col, 0.0)[:, :leads]

    t[...] = rhs[...].astype(F32)
    wlb[...] = (wm[...] * t[...]).astype(BF16)
    loads[1].wait()
    gn[...] = mm(et[...], n_mat[...]).astype(BF16)
    gne[...] = mm(gn[...], el[...]).astype(BF16)
    u[...] = mm(gn[...], wlb[...])
    x[...] = jnp.zeros_like(x)

    def second(e, first_time):
        for slot in SEND_ORDER:
            copy_of(e, slot).wait_recv()
        s1 = (w_e[...] * recv[e].astype(F32)).astype(BF16)
        send[e + 1] = (w_e[...] * (u[...] + mm(gne[...], s1))).astype(BF16)
        for slot in SEND_ORDER:
            copy_of(e + 1, slot).start()
        scaled = (wm[...] * (t[...] + mm(el[...], recv[e]))).astype(BF16)
        x[...] = x[...] + DAMPING * (wm[...] * mm(n_mat[...], scaled))
        if first_time:
            loads[2].wait()
            gs[...] = mm_t(et[...], s_mat[...]).astype(BF16)
            gse[...] = mm(gs[...], el[...]).astype(BF16)
        u[...] = p0[...] - mm(gs[...], x[...].astype(BF16))

    def third(e, first_time):
        for slot in SEND_ORDER:
            copy_of(e, slot).wait_recv()
        send[e + 1] = (u[...] - DAMPING * mm(gse[...], recv[e])).astype(BF16)
        for slot in SEND_ORDER:
            copy_of(e + 1, slot).start()
        x[...] = x[...] + DAMPING * mm(el[...], recv[e])
        if first_time:
            st[...] = jnp.transpose(s_mat[...])
        t[...] = rhs[...].astype(F32) - mm(st[...], x[...].astype(BF16))
        wlb[...] = (wm[...] * t[...]).astype(BF16)
        u[...] = mm(gn[...], wlb[...])

    for step in range(ITERS):
        second(2 * step, step == 0)
        if step < ITERS - 1:
            third(2 * step + 1, step == 0)
    last = 2 * ITERS - 1
    for slot in SEND_ORDER:
        copy_of(last, slot).wait_recv()
    out_ref[0] = x[...] + DAMPING * mm(el[...], recv[last])
    for e in range(2 * ITERS):
        for slot in SEND_ORDER:
            copy_of(e, slot).wait_send()


def body(right_side, schur, neumann, weights, neighbours, counts, shared_rows):
    n = lax.axis_size("sub")
    _, width, leads = right_side.shape
    share = shared_rows.shape[2]
    links = 4 * share
    hbm = pl.BlockSpec(memory_space=pl.ANY)
    vmem = pl.BlockSpec(memory_space=pltpu.VMEM)
    smem = pl.BlockSpec(memory_space=pltpu.SMEM)
    return pl.pallas_call(
        functools.partial(kernel, n),
        out_shape=jax.ShapeDtypeStruct((1, width, leads), F32),
        in_specs=[hbm, hbm, hbm, vmem, smem, smem, vmem],
        out_specs=vmem,
        scratch_shapes=[
            pltpu.VMEM((width, leads), BF16),
            pltpu.VMEM((width, width), BF16),
            pltpu.VMEM((width, width), BF16),
            pltpu.VMEM((width, width), BF16),
            pltpu.VMEM((links, width), BF16),
            pltpu.VMEM((width, links), BF16),
            pltpu.VMEM((links, width), BF16),
            pltpu.VMEM((links, links), BF16),
            pltpu.VMEM((links, width), BF16),
            pltpu.VMEM((links, links), BF16),
            pltpu.VMEM((width, leads), F32),
            pltpu.VMEM((links, leads), F32),
            pltpu.VMEM((links, leads), F32),
            pltpu.VMEM((width, leads), F32),
            pltpu.VMEM((width, leads), F32),
            pltpu.VMEM((links, leads), F32),
            pltpu.VMEM((width, leads), BF16),
            pltpu.VMEM((2 * ITERS, links, leads), BF16),
            pltpu.VMEM((2 * ITERS, links, leads), BF16),
            pltpu.SemaphoreType.DMA((3,)),
            pltpu.SemaphoreType.DMA((2 * ITERS, 4)),
            pltpu.SemaphoreType.DMA((2 * ITERS, 4)),
        ],
        compiler_params=pltpu.CompilerParams(
            collective_id=0, has_side_effects=True, vmem_limit_bytes=48 * 2**20
        ),
    )(right_side, schur, neumann, weights, neighbours, counts, shared_rows)


def solution(mesh):
    in_specs = (
        P("sub", None, None),
        P("sub", None, None),
        P("sub", None, None),
        P("sub", None),
        P("sub", None),
        P("sub"),
        P("sub", None, None),
    )
    return jax.shard_map(body, mesh=mesh, in_specs=in_specs, out_specs=P("sub", None, None), check_vma=False)
```

```python
import functools

import jax
import jax.numpy as jnp
from jax import lax
from jax.experimental import pallas as pl
from jax.experimental.pallas import tpu as pltpu
from jax.sharding import PartitionSpec as P

ITERS = 4
OFFSETS = (1, -1, 16, -16)
OPPOSITE = (1, 0, 3, 2)
DAMPING = 0.7
CHUNKS = 2
F32, BF16 = jnp.float32, jnp.bfloat16


def mm(a, b):
    return jnp.dot(a, b, preferred_element_type=F32)


def mm_t(a, b):
    return lax.dot_general(a, b, (((1,), (1,)), ((), ())), preferred_element_type=F32)


def kernel(
    n, rhs_hbm, s_hbm, n_hbm, w_hbm, nb_hbm, cnt_hbm, rows_hbm, out_ref,
    rhs_in, s_mat, n_mat, w_in, nb_in, cnt_in, rows_in,
    rhs, nt, pick, place, gs, gse, gn, gne, w3, wm, w_e, p0, t, x, u, wlb,
    send, recv, load_sem, send_sem, recv_sem,
):
    leads, width = rhs.shape
    share = rows_in.shape[2]
    me = lax.axis_index("sub")
    partner = [lax.rem(me + (o + n), n) for o in OFFSETS]
    exists = [(me + o >= 0) & (me + o < n) for o in OFFSETS]

    def each(do):
        for slot in range(4):
            pl.when(exists[slot])(functools.partial(do, slot))

    pairs = [
        (rows_hbm, rows_in), (rhs_hbm.at[0], rhs_in), (w_hbm, w_in), (nb_hbm, nb_in),
        (cnt_hbm, cnt_in), (n_hbm.at[0], n_mat), (s_hbm.at[0], s_mat),
    ]
    loads = [pltpu.make_async_copy(a, b, load_sem.at[i]) for i, (a, b) in enumerate(pairs)]
    for copy in loads:
        copy.start()

    barrier = pltpu.get_barrier_semaphore()

    for slot in range(4):
        @pl.when(jnp.logical_not(exists[slot]))
        def _():
            for e in range(2 * ITERS):
                recv[e, slot] = jnp.zeros((leads, share), BF16)

    def greet(slot):
        pl.semaphore_signal(
            barrier, inc=1, device_id=(partner[slot],), device_id_type=pl.DeviceIdType.MESH
        )

    each(greet)

    step_rows = leads // CHUNKS

    def copy_of(e, c, slot, there):
        rows = pl.ds(c * step_rows, step_rows)
        return pltpu.make_async_remote_copy(
            src_ref=send.at[e, slot, rows],
            dst_ref=recv.at[e, there, rows],
            send_sem=send_sem.at[e, c, slot],
            recv_sem=recv_sem.at[e, c, there],
            device_id=(partner[slot],),
            device_id_type=pl.DeviceIdType.MESH,
        )

    def start(e, c):
        each(lambda slot: copy_of(e, c, slot, OPPOSITE[slot]).start())

    def arrive(e, c):
        each(lambda slot: copy_of(e, c, slot, slot).wait_recv())

    def put(e, c, rows):
        for slot in range(4):
            send[e, slot, pl.ds(c * step_rows, step_rows)] = rows[:, slot * share : (slot + 1) * share]

    def got(e, lo, hi):
        return jnp.concatenate([recv[e, slot, lo:hi] for slot in range(4)], axis=1)

    loads[0].wait()
    node_of = lax.broadcasted_iota(jnp.int32, (width, share), 0)
    for slot in range(4):
        hit = node_of == rows_in[0, slot : slot + 1, :]
        pick[:, slot * share : (slot + 1) * share] = hit.astype(F32).astype(BF16)
    loads[1].wait()
    rhs[...] = jnp.transpose(rhs_in[...])
    p0[...] = mm(rhs[...], pick[...])
    for c in range(CHUNKS):
        put(0, c, p0[c * step_rows : (c + 1) * step_rows].astype(BF16))
    pl.semaphore_wait(barrier, sum(jnp.where(there, 1, 0) for there in exists))
    for c in range(CHUNKS):
        start(0, c)

    for i in (2, 3, 4):
        loads[i].wait()
    node = lax.broadcasted_iota(jnp.int32, (1, width), 1)
    w = w_in[...]
    wm[...] = jnp.where(node < cnt_in[0], w, 0.0)
    high = w.astype(BF16)
    rest = w - high.astype(F32)
    middle = rest.astype(BF16)
    low = (rest - middle.astype(F32)).astype(BF16)
    term = lax.broadcasted_iota(jnp.int32, w3.shape, 0)
    w3[...] = jnp.where(
        term == 0, high.astype(F32), jnp.where(term == 1, middle.astype(F32), jnp.where(term == 2, low.astype(F32), 0.0))
    ).astype(BF16)
    w_e[...] = jnp.sum(mm(w3[...], pick[...]), axis=0, keepdims=True)
    lane_of = lax.broadcasted_iota(jnp.int32, (share, width), 1)
    for slot in range(4):
        rows = rows_in[0, slot : slot + 1, :]
        column = jnp.transpose(jnp.broadcast_to(rows, (share, share)))[:, :1]
        live = (nb_in[0, slot] >= 0).astype(F32)
        place[slot * share : (slot + 1) * share, :] = ((lane_of == column).astype(F32) * live).astype(BF16)

    t[...] = rhs[...].astype(F32)
    wlb[...] = (wm[...] * t[...]).astype(BF16)
    loads[5].wait()
    nt[...] = jnp.transpose(n_mat[...])
    gn[...] = mm(nt[...], pick[...]).astype(BF16)
    gne[...] = mm(place[...], gn[...]).astype(BF16)
    u[...] = mm(wlb[...], gn[...])
    x[...] = jnp.zeros_like(x)

    def spans():
        return [(c, c * step_rows, (c + 1) * step_rows) for c in range(CHUNKS)]

    def second(e, first_time):
        for c, lo, hi in spans():
            arrive(e, c)
            s1 = (w_e[...] * got(e, lo, hi).astype(F32)).astype(BF16)
            put(e + 1, c, (w_e[...] * (u[lo:hi] + mm(s1, gne[...]))).astype(BF16))
            start(e + 1, c)
        scaled = (wm[...] * (t[...] + mm(got(e, 0, leads), place[...]))).astype(BF16)
        x[...] = x[...] + DAMPING * (wm[...] * mm(scaled, nt[...]))
        if first_time:
            loads[6].wait()
            gs[...] = mm(s_mat[...], pick[...]).astype(BF16)
            gse[...] = mm(place[...], gs[...]).astype(BF16)

    def third(e):
        u[...] = p0[...] - mm(x[...].astype(BF16), gs[...])
        for c, lo, hi in spans():
            arrive(e, c)
            put(e + 1, c, (u[lo:hi] - DAMPING * mm(got(e, lo, hi), gse[...])).astype(BF16))
            start(e + 1, c)
        x[...] = x[...] + DAMPING * mm(got(e, 0, leads), place[...])
        t[...] = rhs[...].astype(F32) - mm(x[...].astype(BF16), s_mat[...])
        wlb[...] = (wm[...] * t[...]).astype(BF16)
        u[...] = mm(wlb[...], gn[...])

    for step in range(ITERS):
        second(2 * step, step == 0)
        if step < ITERS - 1:
            third(2 * step + 1)
    last = 2 * ITERS - 1
    out_ref[0] = jnp.transpose(x[...])
    for c in range(CHUNKS):
        arrive(last, c)
    kept = jnp.concatenate(
        [recv[last, slot].astype(F32) * (nb_in[0, slot] >= 0).astype(F32) for slot in range(4)], axis=1
    ).astype(BF16)
    out_ref[0] = out_ref[0] + DAMPING * mm_t(pick[...], kept)
    for e in range(2 * ITERS):
        for c in range(CHUNKS):
            each(lambda slot: copy_of(e, c, slot, OPPOSITE[slot]).wait_send())


def body(right_side, schur, neumann, weights, neighbours, counts, shared_rows):
    n = lax.axis_size("sub")
    _, width, leads = right_side.shape
    share = shared_rows.shape[2]
    links = 4 * share
    vmem = pl.BlockSpec(memory_space=pltpu.VMEM)
    return pl.pallas_call(
        functools.partial(kernel, n),
        out_shape=jax.ShapeDtypeStruct((1, width, leads), F32),
        in_specs=[pl.BlockSpec(memory_space=pltpu.HBM)] * 7,
        out_specs=vmem,
        scratch_shapes=[
            pltpu.VMEM((width, leads), BF16),
            pltpu.VMEM((width, width), BF16),
            pltpu.VMEM((width, width), BF16),
            pltpu.VMEM((1, width), F32),
            pltpu.SMEM((1, 4), jnp.int32),
            pltpu.SMEM((1,), jnp.int32),
            pltpu.VMEM((1, 4, share), jnp.int32),
            pltpu.VMEM((leads, width), BF16),
            pltpu.VMEM((width, width), BF16),
            pltpu.VMEM((width, links), BF16),
            pltpu.VMEM((links, width), BF16),
            pltpu.VMEM((width, links), BF16),
            pltpu.VMEM((links, links), BF16),
            pltpu.VMEM((width, links), BF16),
            pltpu.VMEM((links, links), BF16),
            pltpu.VMEM((16, width), BF16),
            pltpu.VMEM((1, width), F32),
            pltpu.VMEM((1, links), F32),
            pltpu.VMEM((leads, links), F32),
            pltpu.VMEM((leads, width), F32),
            pltpu.VMEM((leads, width), F32),
            pltpu.VMEM((leads, links), F32),
            pltpu.VMEM((leads, width), BF16),
            pltpu.VMEM((2 * ITERS, 4, leads, share), BF16),
            pltpu.VMEM((2 * ITERS, 4, leads, share), BF16),
            pltpu.SemaphoreType.DMA((7,)),
            pltpu.SemaphoreType.DMA((2 * ITERS, CHUNKS, 4)),
            pltpu.SemaphoreType.DMA((2 * ITERS, CHUNKS, 4)),
        ],
        compiler_params=pltpu.CompilerParams(
            collective_id=0, has_side_effects=True, vmem_limit_bytes=60 * 2**20
        ),
    )(right_side, schur, neumann, weights, neighbours, counts, shared_rows)


def solution(mesh):
    in_specs = (
        P("sub", None, None),
        P("sub", None, None),
        P("sub", None, None),
        P("sub", None),
        P("sub", None),
        P("sub"),
        P("sub", None, None),
    )
    return jax.shard_map(body, mesh=mesh, in_specs=in_specs, out_specs=P("sub", None, None), check_vma=False)
```

```python
import functools

import jax
import jax.numpy as jnp
from jax import lax
from jax.experimental import pallas as pl
from jax.experimental.pallas import tpu as pltpu
from jax.sharding import PartitionSpec as P

ITERS = 4
OFFSETS = (1, -1, 16, -16)
OPPOSITE = (1, 0, 3, 2)
DAMPING = 0.7
CHUNKS = 2
F32, BF16 = jnp.float32, jnp.bfloat16


def mm(a, b):
    return jnp.dot(a, b, preferred_element_type=F32)


def mm_t(a, b):
    return lax.dot_general(a, b, (((1,), (1,)), ((), ())), preferred_element_type=F32)


def kernel(
    n, rhs_hbm, s_hbm, n_hbm, w_hbm, nb_hbm, cnt_hbm, rows_hbm, out_ref,
    rhs_in, s_mat, n_mat, w_in, nb_in, cnt_in, rows_in,
    rhs, nt, pick, place, gs, gse, gn, gne, w3, wm, w_e, p0, t, x, u, wlb,
    send, recv, load_sem, send_sem, recv_sem,
):
    leads, width = rhs.shape
    share = rows_in.shape[2]
    me = lax.axis_index("sub")
    partner = [lax.rem(me + (o + n), n) for o in OFFSETS]
    exists = [(me + o >= 0) & (me + o < n) for o in OFFSETS]

    def each(do, slots=range(4)):
        for slot in slots:
            pl.when(exists[slot])(functools.partial(do, slot))

    barrier = pltpu.get_barrier_semaphore()

    def greet(slot):
        pl.semaphore_signal(
            barrier, inc=1, device_id=(partner[slot],), device_id_type=pl.DeviceIdType.MESH
        )

    each(greet)

    pairs = [
        (rows_hbm, rows_in), (rhs_hbm.at[0], rhs_in), (w_hbm, w_in), (nb_hbm, nb_in),
        (cnt_hbm, cnt_in), (n_hbm.at[0], n_mat), (s_hbm.at[0], s_mat),
    ]
    loads = [pltpu.make_async_copy(a, b, load_sem.at[i]) for i, (a, b) in enumerate(pairs)]
    for copy in loads:
        copy.start()

    step_rows = leads // CHUNKS

    def copy_of(e, c, slot, there):
        rows = pl.ds(c * step_rows, step_rows)
        return pltpu.make_async_remote_copy(
            src_ref=send.at[e, slot, rows],
            dst_ref=recv.at[e, there, rows],
            send_sem=send_sem.at[e, c, slot],
            recv_sem=recv_sem.at[e, c, there],
            device_id=(partner[slot],),
            device_id_type=pl.DeviceIdType.MESH,
        )

    def start(e, c, slots=range(4)):
        each(lambda slot: copy_of(e, c, slot, OPPOSITE[slot]).start(), slots)

    def arrive(e, c):
        each(lambda slot: copy_of(e, c, slot, slot).wait_recv(), (2, 3, 0, 1))

    def put(e, c, rows, slots=range(4)):
        for i, slot in enumerate(slots):
            send[e, slot, pl.ds(c * step_rows, step_rows)] = rows[:, i * share : (i + 1) * share]

    def got(e, lo, hi):
        return jnp.concatenate([recv[e, slot, lo:hi] for slot in range(4)], axis=1)

    loads[0].wait()
    node_of = lax.broadcasted_iota(jnp.int32, (width, share), 0)
    for slot in range(4):
        hit = node_of == rows_in[0, slot : slot + 1, :]
        pick[:, slot * share : (slot + 1) * share] = hit.astype(F32).astype(BF16)
    loads[1].wait()
    rhs[...] = jnp.transpose(rhs_in[...])
    p0[...] = mm(rhs[...], pick[...])
    for c in range(CHUNKS):
        put(0, c, p0[c * step_rows : (c + 1) * step_rows].astype(BF16))
    pl.semaphore_wait(barrier, sum(jnp.where(there, 1, 0) for there in exists))
    for c in range(CHUNKS):
        start(0, c)

    for slot in range(4):
        @pl.when(jnp.logical_not(exists[slot]))
        def _():
            for e in range(2 * ITERS):
                recv[e, slot] = jnp.zeros((leads, share), BF16)

    for i in (2, 3, 4):
        loads[i].wait()
    node = lax.broadcasted_iota(jnp.int32, (1, width), 1)
    w = w_in[...]
    wm[...] = jnp.where(node < cnt_in[0], w, 0.0)
    high = w.astype(BF16)
    rest = w - high.astype(F32)
    middle = rest.astype(BF16)
    low = (rest - middle.astype(F32)).astype(BF16)
    term = lax.broadcasted_iota(jnp.int32, w3.shape, 0)
    w3[...] = jnp.where(
        term == 0, high.astype(F32), jnp.where(term == 1, middle.astype(F32), jnp.where(term == 2, low.astype(F32), 0.0))
    ).astype(BF16)
    w_e[...] = jnp.sum(mm(w3[...], pick[...]), axis=0, keepdims=True)
    lane_of = lax.broadcasted_iota(jnp.int32, (share, width), 1)
    for slot in range(4):
        rows = rows_in[0, slot : slot + 1, :]
        column = jnp.transpose(jnp.broadcast_to(rows, (share, share)))[:, :1]
        live = (nb_in[0, slot] >= 0).astype(F32)
        place[slot * share : (slot + 1) * share, :] = ((lane_of == column).astype(F32) * live).astype(BF16)

    t[...] = rhs[...].astype(F32)
    wlb[...] = (wm[...] * t[...]).astype(BF16)
    loads[5].wait()
    nt[...] = jnp.transpose(n_mat[...])
    gn[...] = mm(nt[...], pick[...]).astype(BF16)
    gne[...] = mm(place[...], gn[...]).astype(BF16)
    u[...] = mm(wlb[...], gn[...])
    x[...] = jnp.zeros_like(x)

    def spans():
        return [(c, c * step_rows, (c + 1) * step_rows) for c in range(CHUNKS)]

    halves = [((0, 1), slice(0, 2 * share)), ((2, 3), slice(2 * share, 4 * share))]

    def second(e, first_time):
        for c, lo, hi in spans():
            arrive(e, c)
            s1 = (w_e[...] * got(e, lo, hi).astype(F32)).astype(BF16)
            for slots, at in halves:
                put(e + 1, c, (w_e[:, at] * (u[lo:hi, at] + mm(s1, gne[:, at]))).astype(BF16), slots)
                start(e + 1, c, slots)
        scaled = (wm[...] * (t[...] + mm(got(e, 0, leads), place[...]))).astype(BF16)
        x[...] = x[...] + DAMPING * (wm[...] * mm(scaled, nt[...]))
        if first_time:
            loads[6].wait()
            gs[...] = mm(s_mat[...], pick[...]).astype(BF16)
            gse[...] = mm(place[...], gs[...]).astype(BF16)

    def third(e):
        u[...] = p0[...] - mm(x[...].astype(BF16), gs[...])
        for c, lo, hi in spans():
            arrive(e, c)
            arrived = got(e, lo, hi)
            for slots, at in halves:
                put(e + 1, c, (u[lo:hi, at] - DAMPING * mm(arrived, gse[:, at])).astype(BF16), slots)
                start(e + 1, c, slots)
        x[...] = x[...] + DAMPING * mm(got(e, 0, leads), place[...])
        t[...] = rhs[...].astype(F32) - mm(x[...].astype(BF16), s_mat[...])
        wlb[...] = (wm[...] * t[...]).astype(BF16)
        u[...] = mm(wlb[...], gn[...])

    for step in range(ITERS):
        second(2 * step, step == 0)
        if step < ITERS - 1:
            third(2 * step + 1)
    last = 2 * ITERS - 1
    out_ref[0] = jnp.transpose(x[...])
    for c in range(CHUNKS):
        arrive(last, c)
    kept = jnp.concatenate(
        [recv[last, slot].astype(F32) * (nb_in[0, slot] >= 0).astype(F32) for slot in range(4)], axis=1
    ).astype(BF16)
    out_ref[0] = out_ref[0] + DAMPING * mm_t(pick[...], kept)
    for e in range(2 * ITERS):
        for c in range(CHUNKS):
            each(lambda slot: copy_of(e, c, slot, OPPOSITE[slot]).wait_send())


def in_hbm(*arrays):
    return [pltpu.with_memory_space_constraint(a, pltpu.HBM) for a in arrays]


def body(right_side, schur, neumann, weights, neighbours, counts, shared_rows):
    n = lax.axis_size("sub")
    _, width, leads = right_side.shape
    share = shared_rows.shape[2]
    links = 4 * share
    vmem = pl.BlockSpec(memory_space=pltpu.VMEM)
    return pl.pallas_call(
        functools.partial(kernel, n),
        out_shape=jax.ShapeDtypeStruct((1, width, leads), F32),
        in_specs=[pl.BlockSpec(memory_space=pltpu.HBM)] * 7,
        out_specs=vmem,
        scratch_shapes=[
            pltpu.VMEM((width, leads), BF16),
            pltpu.VMEM((width, width), BF16),
            pltpu.VMEM((width, width), BF16),
            pltpu.VMEM((1, width), F32),
            pltpu.SMEM((1, 4), jnp.int32),
            pltpu.SMEM((1,), jnp.int32),
            pltpu.VMEM((1, 4, share), jnp.int32),
            pltpu.VMEM((leads, width), BF16),
            pltpu.VMEM((width, width), BF16),
            pltpu.VMEM((width, links), BF16),
            pltpu.VMEM((links, width), BF16),
            pltpu.VMEM((width, links), BF16),
            pltpu.VMEM((links, links), BF16),
            pltpu.VMEM((width, links), BF16),
            pltpu.VMEM((links, links), BF16),
            pltpu.VMEM((16, width), BF16),
            pltpu.VMEM((1, width), F32),
            pltpu.VMEM((1, links), F32),
            pltpu.VMEM((leads, links), F32),
            pltpu.VMEM((leads, width), F32),
            pltpu.VMEM((leads, width), F32),
            pltpu.VMEM((leads, links), F32),
            pltpu.VMEM((leads, width), BF16),
            pltpu.VMEM((2 * ITERS, 4, leads, share), BF16),
            pltpu.VMEM((2 * ITERS, 4, leads, share), BF16),
            pltpu.SemaphoreType.DMA((7,)),
            pltpu.SemaphoreType.DMA((2 * ITERS, CHUNKS, 4)),
            pltpu.SemaphoreType.DMA((2 * ITERS, CHUNKS, 4)),
        ],
        compiler_params=pltpu.CompilerParams(
            collective_id=0, has_side_effects=True, vmem_limit_bytes=48 * 2**20
        ),
    )(*in_hbm(right_side, schur, neumann, weights, neighbours), counts, *in_hbm(shared_rows))


def solution(mesh):
    in_specs = (
        P("sub", None, None),
        P("sub", None, None),
        P("sub", None, None),
        P("sub", None),
        P("sub", None),
        P("sub"),
        P("sub", None, None),
    )
    return jax.shard_map(body, mesh=mesh, in_specs=in_specs, out_specs=P("sub", None, None), check_vma=False)
```

```python
import functools

import jax
import jax.numpy as jnp
from jax import lax
from jax.experimental import pallas as pl
from jax.experimental.pallas import tpu as pltpu
from jax.sharding import PartitionSpec as P

ITERS = 4
OFFSETS = (1, -1, 16, -16)
OPPOSITE = (1, 0, 3, 2)
DAMPING = 0.7
CHUNKS = 2
F32, BF16 = jnp.float32, jnp.bfloat16


def mm(a, b):
    return jnp.dot(a, b, preferred_element_type=F32)


def mm_t(a, b):
    return lax.dot_general(a, b, (((1,), (1,)), ((), ())), preferred_element_type=F32)


def kernel(
    n, rhs_hbm, s_hbm, n_hbm, w_hbm, nb_hbm, cnt_hbm, rows_hbm, out_ref,
    rhs_in, s_mat, n_mat, w_in, nb_in, cnt_in, rows_in,
    rhs, nt, pick, place, gs, gse, gn, gne, w3, wm, w_e, p0, t, x, u, wlb,
    send, recv, load_sem, send_sem, recv_sem,
):
    leads, width = rhs.shape
    share = rows_in.shape[2]
    me = lax.axis_index("sub")
    partner = [lax.rem(me + (o + n), n) for o in OFFSETS]
    exists = [(me + o >= 0) & (me + o < n) for o in OFFSETS]

    def each(do, slots=range(4)):
        for slot in slots:
            pl.when(exists[slot])(functools.partial(do, slot))

    barrier = pltpu.get_barrier_semaphore()

    def greet(slot):
        pl.semaphore_signal(
            barrier, inc=1, device_id=(partner[slot],), device_id_type=pl.DeviceIdType.MESH
        )

    each(greet)

    pairs = [
        (rows_hbm, rows_in), (rhs_hbm.at[0], rhs_in), (w_hbm, w_in), (nb_hbm, nb_in),
        (cnt_hbm, cnt_in), (n_hbm.at[0], n_mat), (s_hbm.at[0], s_mat),
    ]
    loads = [pltpu.make_async_copy(a, b, load_sem.at[i]) for i, (a, b) in enumerate(pairs)]
    for copy in loads:
        copy.start()

    cuts = (0, 48, leads)

    def copy_of(e, c, slot, there):
        rows = pl.ds(cuts[c], cuts[c + 1] - cuts[c])
        return pltpu.make_async_remote_copy(
            src_ref=send.at[e, slot, rows],
            dst_ref=recv.at[e, there, rows],
            send_sem=send_sem.at[e, c, slot],
            recv_sem=recv_sem.at[e, c, there],
            device_id=(partner[slot],),
            device_id_type=pl.DeviceIdType.MESH,
        )

    def start(e, c, slots=range(4)):
        each(lambda slot: copy_of(e, c, slot, OPPOSITE[slot]).start(), slots)

    def arrive(e, c):
        each(lambda slot: copy_of(e, c, slot, slot).wait_recv(), (2, 3, 0, 1))

    def put(e, c, rows, slots=range(4)):
        for i, slot in enumerate(slots):
            send[e, slot, cuts[c] : cuts[c + 1]] = rows[:, i * share : (i + 1) * share]

    def got(e, lo, hi):
        return jnp.concatenate([recv[e, slot, lo:hi] for slot in range(4)], axis=1)

    loads[0].wait()
    node_of = lax.broadcasted_iota(jnp.int32, (width, share), 0)
    for slot in range(4):
        hit = node_of == rows_in[0, slot : slot + 1, :]
        pick[:, slot * share : (slot + 1) * share] = hit.astype(F32).astype(BF16)
    loads[1].wait()
    rhs[...] = jnp.transpose(rhs_in[...])
    p0[...] = mm(rhs[...], pick[...])
    for c in range(CHUNKS):
        put(0, c, p0[cuts[c] : cuts[c + 1]].astype(BF16))
    pl.semaphore_wait(barrier, sum(jnp.where(there, 1, 0) for there in exists))
    for c in range(CHUNKS):
        start(0, c)

    for slot in range(4):
        @pl.when(jnp.logical_not(exists[slot]))
        def _():
            for e in range(2 * ITERS):
                recv[e, slot] = jnp.zeros((leads, share), BF16)

    for i in (2, 3, 4):
        loads[i].wait()
    node = lax.broadcasted_iota(jnp.int32, (1, width), 1)
    w = w_in[...]
    wm[...] = jnp.where(node < cnt_in[0], w, 0.0)
    high = w.astype(BF16)
    rest = w - high.astype(F32)
    middle = rest.astype(BF16)
    low = (rest - middle.astype(F32)).astype(BF16)
    term = lax.broadcasted_iota(jnp.int32, w3.shape, 0)
    w3[...] = jnp.where(
        term == 0, high.astype(F32), jnp.where(term == 1, middle.astype(F32), jnp.where(term == 2, low.astype(F32), 0.0))
    ).astype(BF16)
    w_e[...] = jnp.sum(mm(w3[...], pick[...]), axis=0, keepdims=True)
    lane_of = lax.broadcasted_iota(jnp.int32, (share, width), 1)
    for slot in range(4):
        rows = rows_in[0, slot : slot + 1, :]
        column = jnp.transpose(jnp.broadcast_to(rows, (share, share)))[:, :1]
        live = (nb_in[0, slot] >= 0).astype(F32)
        place[slot * share : (slot + 1) * share, :] = ((lane_of == column).astype(F32) * live).astype(BF16)

    t[...] = rhs[...].astype(F32)
    wlb[...] = (wm[...] * t[...]).astype(BF16)
    loads[5].wait()
    nt[...] = jnp.transpose(n_mat[...])
    gn[...] = mm(nt[...], pick[...]).astype(BF16)
    gne[...] = mm(place[...], gn[...]).astype(BF16)
    u[...] = mm(wlb[...], gn[...])
    x[...] = jnp.zeros_like(x)

    def spans():
        return [(c, cuts[c], cuts[c + 1]) for c in range(CHUNKS)]

    halves = [((0, 1), slice(0, 2 * share)), ((2, 3), slice(2 * share, 4 * share))]

    def second(e, first_time):
        for c, lo, hi in spans():
            arrive(e, c)
            s1 = (w_e[...] * got(e, lo, hi).astype(F32)).astype(BF16)
            for slots, at in halves:
                put(e + 1, c, (w_e[:, at] * (u[lo:hi, at] + mm(s1, gne[:, at]))).astype(BF16), slots)
                start(e + 1, c, slots)
        scaled = (wm[...] * (t[...] + mm(got(e, 0, leads), place[...]))).astype(BF16)
        x[...] = x[...] + DAMPING * (wm[...] * mm(scaled, nt[...]))
        if first_time:
            loads[6].wait()
            gs[...] = mm(s_mat[...], pick[...]).astype(BF16)
            gse[...] = mm(place[...], gs[...]).astype(BF16)

    def third(e):
        u[...] = p0[...] - mm(x[...].astype(BF16), gs[...])
        for c, lo, hi in spans():
            arrive(e, c)
            arrived = got(e, lo, hi)
            for slots, at in halves:
                put(e + 1, c, (u[lo:hi, at] - DAMPING * mm(arrived, gse[:, at])).astype(BF16), slots)
                start(e + 1, c, slots)
        x[...] = x[...] + DAMPING * mm(got(e, 0, leads), place[...])
        t[...] = rhs[...].astype(F32) - mm(x[...].astype(BF16), s_mat[...])
        wlb[...] = (wm[...] * t[...]).astype(BF16)
        u[...] = mm(wlb[...], gn[...])

    for step in range(ITERS):
        second(2 * step, step == 0)
        if step < ITERS - 1:
            third(2 * step + 1)
    last = 2 * ITERS - 1
    out_ref[0] = jnp.transpose(x[...])
    for c in range(CHUNKS):
        arrive(last, c)
    kept = jnp.concatenate(
        [recv[last, slot].astype(F32) * (nb_in[0, slot] >= 0).astype(F32) for slot in range(4)], axis=1
    ).astype(BF16)
    out_ref[0] = out_ref[0] + DAMPING * mm_t(pick[...], kept)
    for e in range(2 * ITERS):
        for c in range(CHUNKS):
            each(lambda slot: copy_of(e, c, slot, OPPOSITE[slot]).wait_send())


def in_hbm(*arrays):
    return [pltpu.with_memory_space_constraint(a, pltpu.HBM) for a in arrays]


def body(right_side, schur, neumann, weights, neighbours, counts, shared_rows):
    n = lax.axis_size("sub")
    _, width, leads = right_side.shape
    share = shared_rows.shape[2]
    links = 4 * share
    vmem = pl.BlockSpec(memory_space=pltpu.VMEM)
    return pl.pallas_call(
        functools.partial(kernel, n),
        out_shape=jax.ShapeDtypeStruct((1, width, leads), F32),
        in_specs=[pl.BlockSpec(memory_space=pltpu.HBM)] * 7,
        out_specs=vmem,
        scratch_shapes=[
            pltpu.VMEM((width, leads), BF16),
            pltpu.VMEM((width, width), BF16),
            pltpu.VMEM((width, width), BF16),
            pltpu.VMEM((1, width), F32),
            pltpu.SMEM((1, 4), jnp.int32),
            pltpu.SMEM((1,), jnp.int32),
            pltpu.VMEM((1, 4, share), jnp.int32),
            pltpu.VMEM((leads, width), BF16),
            pltpu.VMEM((width, width), BF16),
            pltpu.VMEM((width, links), BF16),
            pltpu.VMEM((links, width), BF16),
            pltpu.VMEM((width, links), BF16),
            pltpu.VMEM((links, links), BF16),
            pltpu.VMEM((width, links), BF16),
            pltpu.VMEM((links, links), BF16),
            pltpu.VMEM((16, width), BF16),
            pltpu.VMEM((1, width), F32),
            pltpu.VMEM((1, links), F32),
            pltpu.VMEM((leads, links), F32),
            pltpu.VMEM((leads, width), F32),
            pltpu.VMEM((leads, width), F32),
            pltpu.VMEM((leads, links), F32),
            pltpu.VMEM((leads, width), BF16),
            pltpu.VMEM((2 * ITERS, 4, leads, share), BF16),
            pltpu.VMEM((2 * ITERS, 4, leads, share), BF16),
            pltpu.SemaphoreType.DMA((7,)),
            pltpu.SemaphoreType.DMA((2 * ITERS, CHUNKS, 4)),
            pltpu.SemaphoreType.DMA((2 * ITERS, CHUNKS, 4)),
        ],
        compiler_params=pltpu.CompilerParams(
            collective_id=0, has_side_effects=True, vmem_limit_bytes=48 * 2**20
        ),
    )(*in_hbm(right_side, schur, neumann, weights, neighbours), counts, *in_hbm(shared_rows))


def solution(mesh):
    in_specs = (
        P("sub", None, None),
        P("sub", None, None),
        P("sub", None, None),
        P("sub", None),
        P("sub", None),
        P("sub"),
        P("sub", None, None),
    )
    return jax.shard_map(body, mesh=mesh, in_specs=in_specs, out_specs=P("sub", None, None), check_vma=False)
```
